256 devices in a mesh: row: 32 (over y_lo, z, core), col: 8 (over y_hi, x).
Axes of the slice: x: 4, y: 4 (y_hi: 2, y_lo: 2; y = y_hi * 2 + y_lo), z: 8, core: 2. Of those that a mesh axis runs over, the one named last changes fastest.
Arguments:
- left_slots: float32 [32, 4096, 512], P('row', 'col'), may hold values from -0.109375 to 0.109375
- right: float32 [8192, 8192], P('col', 'row'), may hold values from -6 to 6
- previous: float32 [4096, 8192], P('col', 'row'), may hold values from -4 to 4
- offsets: int32 [6], replicated, may hold values from 0 to 15, as said below
- owners: int32 [8, 6], P('col'), may hold values from 0 to 31, as said below
Outputs:
- next_density: float32 [4096, 8192], P('col', 'row')
The draws below stay inside these ranges and needn't reach their ends.
Inputs may be any that keep to these rules, and one draw needn't show every extreme that they name: `offsets`: distinct, in any order; they include 0 and 15. `owners`: distinct within each grid row.
All inputs are finite; a program needn't handle non-finite values.
Results may differ from the reference program's by a relative error of at most 0.0001.
Values sent between devices are 32-bit elements; how exact they have to be, the bound alone decides.
A program may use at most 64 MiB of HBM per device.

```python
import jax
import jax.numpy as jnp
from jax import lax

KW = 512
KB_PER = 2
ROWS_DEV = 512
KBL = 16
NDIAG = 6
KDIM = 8192
ROWS = 4096
COLS = 8192
N_ROW = 32
N_COL = 8


def draw_offsets(key, part):
    inner = jax.random.permutation(jax.random.fold_in(key, 11), KBL - 2) + 1
    chosen = jnp.concatenate([jnp.zeros((1,), jnp.int32), inner[:NDIAG - 2].astype(jnp.int32), jnp.full((1,), KBL - 1, jnp.int32)])
    order = jax.random.permutation(jax.random.fold_in(key, 37), NDIAG)
    return chosen[order].astype(jnp.int32)


def draw_owners(key, part):
    used = min(N_COL * NDIAG, N_ROW)
    rest = (jax.random.permutation(jax.random.fold_in(key, 23), N_ROW - 2) + 1).astype(jnp.int32)
    order = jnp.concatenate([jnp.full((1,), N_ROW - 1, jnp.int32), jnp.zeros((1,), jnp.int32), rest])
    offset_shift = jax.random.randint(jax.random.fold_in(key, 29), (), 0, used - 1)
    order = jnp.roll(order, offset_shift)
    where_at = (jnp.arange(N_COL)[:, None] * NDIAG + jnp.arange(NDIAG)[None, :]) % N_ROW
    return order[where_at].astype(jnp.int32)


def shard_levels(key, shape, split, smallest, top_value):
    def one(position, parts):
        heights = jax.random.uniform(jax.random.fold_in(jax.random.fold_in(key, 6), position), (parts,), jnp.float32, smallest / len(split), top_value / len(split))
        return jnp.repeat(jnp.exp(heights), shape[position] // parts).reshape((-1,) + (1,) * (len(shape) - position - 1))

    factor_of = one(*split[0])
    for cut in split[1:]:
        factor_of = factor_of * one(*cut)
    return factor_of


def centred(own_key, dims, width, reach, cuts=(), dtype=jnp.bfloat16):
    array = width * jax.random.normal(own_key, dims, jnp.float32)
    if cuts:
        array = array * shard_levels(own_key, dims, cuts, -0.22, 0.18)
    return jnp.clip(array, -reach, reach).astype(dtype)


def setup_inputs(seed: int = 0) -> dict:
    key_list = jax.random.split(jax.random.key(seed), 6)
    left_slots = centred(key_list[0], (N_ROW, ROWS, KW), (NDIAG * KW) ** -0.5, 0.109375, ((0, 32), (1, 8)), jnp.float32)
    right = centred(key_list[1], (KDIM, COLS), 1.0, 6.0, ((0, 8), (1, 32)), jnp.float32)
    previous = centred(key_list[2], (ROWS, COLS), 0.5, 4.0, ((0, 8), (1, 32)), jnp.float32)
    offsets = draw_offsets(jax.random.fold_in(key_list[5], 71), 0)
    owners = draw_owners(jax.random.fold_in(key_list[5], 71), 0)
    return {"left_slots": left_slots, "right": right, "previous": previous, "offsets": offsets, "owners": owners}


def reference(left_slots, right, previous, offsets, owners):
    row_parts = []
    for grid_row in range(N_COL):
        partial_sum = jnp.zeros((ROWS_DEV, right.shape[1]), jnp.float32)
        for number in range(NDIAG):
            holder = owners[grid_row, number]
            slab = lax.dynamic_index_in_dim(left_slots, holder.astype(jnp.int32), 0, keepdims=False)
            slab = slab[grid_row * ROWS_DEV:(grid_row + 1) * ROWS_DEV, :]
            block = (KB_PER * grid_row + offsets[number]) % KBL
            piece = lax.dynamic_slice_in_dim(right, (block * KW).astype(jnp.int32), KW, 0)
            partial_sum = partial_sum + jnp.dot(slab, piece, precision=lax.Precision.HIGHEST, preferred_element_type=jnp.float32)
        row_parts.append(partial_sum)
    product = jnp.concatenate(row_parts, axis=0)
    return 2.0 * previous - product
```

```python
import functools

import jax
import jax.numpy as jnp
from jax import lax
from jax.experimental import pallas as pl
from jax.experimental.pallas import tpu as pltpu
from jax.sharding import PartitionSpec as P

NY, NZ, NC = 2, 8, 2
NROW = NY * NZ * NC
NH, NX = 2, 4
ND = 6
KW = 512
COLS = 256
CH = KW // NROW
QUAD = NY * NC * CH
HALF = ND // 2


def chunk_of(zz, yy, cc):
    return (zz * NY + yy) * NC + cc


def row_of(zz, yy, cc):
    return (yy * NZ + zz) * NC + cc


def kernel(
    offsets,
    owners,
    left,
    right,
    out,
    spread,
    chosen,
    partner_chosen,
    gathered,
    rights,
    right_hi,
    right_lo,
    own_sum,
    other_sum,
    send_par,
    recv_par,
    spread_send,
    spread_recv,
    swap_sem,
    right_send,
    right_recv,
    local_sem,
    gather_send,
    gather_recv,
    par_send,
    par_recv,
):
    row = lax.axis_index("row")
    col = lax.axis_index("col")
    y = row // (NZ * NC)
    z = (row // NC) % NZ
    c = row % NC
    h = col // NX
    x = col % NX
    mine = chunk_of(z, y, c)
    east = h * NX + (x + 1) % NX
    west = h * NX + (x + NX - 1) % NX
    partner = (1 - h) * NX + x

    barrier = pltpu.get_barrier_semaphore()

    def greet(step, carry):
        pl.semaphore_signal(barrier, inc=1, device_id={"row": (row + step) % NROW})
        return carry

    lax.fori_loop(1, NROW, greet, 0)
    for where in (east, west, partner):
        pl.semaphore_signal(barrier, inc=1, device_id={"col": where})
    pl.semaphore_wait(barrier, NROW - 1 + 3)

    def right_copy(source_ref, owner, slot, way, where):
        return pltpu.make_async_remote_copy(
            src_ref=source_ref,
            dst_ref=rights.at[owner, slot],
            send_sem=right_send.at[way, slot],
            recv_sem=right_recv.at[owner, slot],
            device_id={"col": where},
        )

    first = []
    for slot_east, slot_west in ((0, 1), (1, 0)):
        for way, slot, where in ((0, slot_east, east), (1, slot_west, west)):
            copy = right_copy(right.at[slot], x, slot, way, where)
            copy.start()
            first.append(copy)

    def spread_copy(step):
        peer = (row + step) % NROW
        py = peer // (NZ * NC)
        pz = (peer // NC) % NZ
        pc = peer % NC
        begin = pl.multiple_of(chunk_of(pz, py, pc) * CH, CH)
        return pltpu.make_async_remote_copy(
            src_ref=left.at[pl.ds(begin, CH)],
            dst_ref=spread.at[row],
            send_sem=spread_send.at[step],
            recv_sem=spread_recv.at[row],
            device_id={"row": peer},
        )

    def spread_start(step, carry):
        spread_copy(step).start()
        return carry

    lax.fori_loop(1, NROW, spread_start, 0)
    local = pltpu.make_async_copy(right, rights.at[x], local_sem.at[0])
    local.start()
    own_begin = pl.multiple_of(mine * CH, CH)
    spread[row] = left[pl.ds(own_begin, CH), :]

    def spread_done(step, carry):
        peer = (row + step) % NROW
        pltpu.make_async_remote_copy(
            src_ref=spread.at[peer],
            dst_ref=spread.at[peer],
            send_sem=spread_send.at[step],
            recv_sem=spread_recv.at[peer],
            device_id={"row": peer},
        ).wait_recv()
        return carry

    lax.fori_loop(1, NROW, spread_done, 0)

    for number in range(ND):
        chosen[number] = spread[owners[0, number]]
    swap = pltpu.make_async_remote_copy(
        src_ref=chosen,
        dst_ref=partner_chosen,
        send_sem=swap_sem.at[0],
        recv_sem=swap_sem.at[1],
        device_id={"col": partner},
    )
    swap.start()
    shift = [offsets[number] // 2 for number in range(ND)]
    parity = [offsets[number] % 2 for number in range(ND)]
    crossed = [((x + shift[number]) // NX) % 2 for number in range(ND)]
    swap.wait_recv()
    for number in range(ND):
        gathered[mine, number] = jnp.where(
            crossed[number] == 1, partner_chosen[number], chosen[number]
        )

    beside = {"row": row_of(z, y, 1 - c)}
    across = {"row": row_of(z, 1 - y, c)}
    up = {"row": row_of((z + 1) % NZ, y, c)}
    down = {"row": row_of((z + NZ - 1) % NZ, y, c)}
    BESIDE, ACROSS, UP, DOWN = 0, 1, 2, 3
    targets = {BESIDE: beside, ACROSS: across, UP: up, DOWN: down}
    sent = {BESIDE: 0, ACROSS: 0, UP: 0, DOWN: 0}

    def unit_copy(zz, yy, cc, part, way):
        chunk = chunk_of(zz, yy, cc)
        ref = gathered.at[chunk, pl.ds(part * HALF, HALF)]
        return pltpu.make_async_remote_copy(
            src_ref=ref,
            dst_ref=ref,
            send_sem=gather_send.at[way],
            recv_sem=gather_recv.at[chunk, part],
            device_id=targets[way],
        )

    def send(zz, yy, cc, part, *ways):
        for way in ways:
            sent[way] += 1
            unit_copy(zz, yy, cc, part, way).start()

    def receive(zz, yy, cc, part):
        unit_copy(zz, yy, cc, part, BESIDE).wait_recv()

    send(z, y, c, 0, ACROSS, UP, DOWN)
    send(z, y, c, 1, UP, DOWN, ACROSS)
    send(z, y, c, 0, BESIDE)
    send(z, y, c, 1, BESIDE)
    receive(z, 1 - y, c, 0)
    send(z, 1 - y, c, 0, UP, DOWN, BESIDE)

    def right_wait(owner, slot):
        right_copy(rights.at[owner, slot], owner, slot, 0, east).wait_recv()

    x_west = (x + NX - 1) % NX
    x_east = (x + 1) % NX
    x_far = (x + 2) % NX
    right_wait(x_west, 0)
    relay_east = right_copy(rights.at[x_west, 0], x_west, 0, 2, east)
    relay_east.start()
    right_wait(x_east, 1)
    relay_west = right_copy(rights.at[x_east, 1], x_east, 1, 2, west)
    relay_west.start()

    def z_stage(step):
        below = (z + NZ - step) % NZ
        above = (z + step) % NZ
        far = step == NZ // 2
        last = step == NZ // 2 - 1
        todo = []
        for yy, part in ((y, 0), (y, 1), (1 - y, 0)):
            extra = (ACROSS, BESIDE) if part == 1 else (BESIDE,)
            if not (far and part == 1):
                on = () if far or (last and part == 1) else (UP,)
                todo.append((below, yy, part, on + extra))
            if not (far and part == 0):
                on = () if far or (last and part == 0) else (DOWN,)
                todo.append((above, yy, part, on + extra))
        for zz, yy, part, ways in todo:
            receive(zz, yy, c, part)
            send(zz, yy, c, part, *ways)

    def places(step):
        if step == 0:
            return (z,)
        if step == NZ // 2:
            return ((z + step) % NZ,)
        return ((z + NZ - step) % NZ, (z + step) % NZ)

    def y_stage(step):
        for zz in places(step):
            receive(zz, 1 - y, c, 1)
            send(zz, 1 - y, c, 1, BESIDE)

    def par_copy(zz):
        return pltpu.make_async_remote_copy(
            src_ref=send_par.at[zz],
            dst_ref=recv_par.at[zz],
            send_sem=par_send.at[zz],
            recv_sem=par_recv.at[zz],
            device_id={"col": partner},
        )

    def multiply_stage(step):
        spots = places(step)
        for zz in spots:
            for yy in (0, 1):
                for part in (0, 1):
                    receive(zz, yy, 1 - c, part)
        rows = QUAD * len(spots)
        for number in range(ND):
            pieces = []
            for zz in spots:
                begin = zz * NY * NC
                pieces.append(
                    gathered[pl.ds(begin, NY * NC), number].reshape(QUAD, KW)
                )
            block = pieces[0] if len(pieces) == 1 else jnp.concatenate(pieces, axis=0)
            hi = block.astype(jnp.bfloat16)
            lo = (block - hi.astype(jnp.float32)).astype(jnp.bfloat16)
            rhi = right_hi[number]
            rlo = right_lo[number]
            term = jnp.dot(hi, rhi, preferred_element_type=jnp.float32)
            term += jnp.dot(hi, rlo, preferred_element_type=jnp.float32)
            term += jnp.dot(lo, rhi, preferred_element_type=jnp.float32)
            zero = jnp.zeros_like(term)
            other = jnp.where(crossed[number] == 1, term, zero)
            here = jnp.where(crossed[number] == 1, zero, term)
            if number == 0:
                own_sum[pl.ds(0, rows)] = here
                other_sum[pl.ds(0, rows)] = other
            else:
                own_sum[pl.ds(0, rows)] += here
                other_sum[pl.ds(0, rows)] += other
        for index, zz in enumerate(spots):
            send_par[zz] = other_sum[index * QUAD : (index + 1) * QUAD]
            par_copy(zz).start()
            begin = pl.multiple_of(zz * QUAD, QUAD)
            out[pl.ds(begin, QUAD)] = own_sum[index * QUAD : (index + 1) * QUAD]

    def finish_stage(step):
        for zz in places(step):
            par_copy(zz).wait_recv()
            begin = pl.multiple_of(zz * QUAD, QUAD)
            out[pl.ds(begin, QUAD)] += recv_par[zz]

    def prepare_right():
        local.wait()
        right_wait(x_west, 1)
        right_wait(x_east, 0)
        right_wait(x_far, 0)
        right_wait(x_far, 1)
        for number in range(ND):
            block = rights[(x + shift[number]) % NX, parity[number]]
            hi = block.astype(jnp.bfloat16)
            right_hi[number] = hi
            right_lo[number] = (block - hi.astype(jnp.float32)).astype(jnp.bfloat16)

    z_stage(1)
    y_stage(0)
    z_stage(2)
    y_stage(1)
    z_stage(3)
    prepare_right()
    y_stage(2)
    multiply_stage(0)
    multiply_stage(1)
    z_stage(4)
    y_stage(3)
    multiply_stage(2)
    finish_stage(0)
    finish_stage(1)
    y_stage(4)
    multiply_stage(3)
    finish_stage(2)
    multiply_stage(4)
    finish_stage(3)
    finish_stage(4)

    def spread_sent(step, carry):
        spread_copy(step).wait_send()
        return carry

    lax.fori_loop(1, NROW, spread_sent, 0)
    for copy in first + [relay_east, relay_west, swap]:
        copy.wait_send()
    for zz in range(NZ):
        par_copy(zz).wait_send()
    for way in targets:
        ref = gathered.at[pl.ds(0, sent[way]), pl.ds(0, HALF)]
        pltpu.make_async_remote_copy(
            src_ref=ref,
            dst_ref=ref,
            send_sem=gather_send.at[way],
            recv_sem=gather_recv.at[0, 0],
            device_id=targets[way],
        ).wait_send()


def shards(left_slots, right, previous, offsets, owners):
    f32 = jnp.float32
    vmem = pl.BlockSpec(memory_space=pltpu.VMEM)
    smem = pl.BlockSpec(memory_space=pltpu.SMEM)
    dma = pltpu.SemaphoreType.DMA
    total = pl.pallas_call(
        kernel,
        out_shape=jax.ShapeDtypeStruct((KW, COLS), f32),
        in_specs=[smem, smem, vmem, vmem],
        out_specs=vmem,
        scratch_shapes=[
            pltpu.VMEM((NROW, CH, KW), f32),
            pltpu.VMEM((ND, CH, KW), f32),
            pltpu.VMEM((ND, CH, KW), f32),
            pltpu.VMEM((NROW, ND, CH, KW), f32),
            pltpu.VMEM((NX, 2, KW, COLS), f32),
            pltpu.VMEM((ND, KW, COLS), jnp.bfloat16),
            pltpu.VMEM((ND, KW, COLS), jnp.bfloat16),
            pltpu.VMEM((2 * QUAD, COLS), f32),
            pltpu.VMEM((2 * QUAD, COLS), f32),
            pltpu.VMEM((NZ, QUAD, COLS), f32),
            pltpu.VMEM((NZ, QUAD, COLS), f32),
            dma((NROW,)),
            dma((NROW,)),
            dma((2,)),
            dma((3, 2)),
            dma((NX, 2)),
            dma((1,)),
            dma((4,)),
            dma((NROW, 2)),
            dma((NZ,)),
            dma((NZ,)),
        ],
        compiler_params=pltpu.CompilerParams(
            collective_id=0, has_side_effects=True, vmem_limit_bytes=48 * 1024 * 1024
        ),
    )(offsets, owners, left_slots[0], right.reshape(2, KW, COLS))
    return 2.0 * previous - total


def solution(mesh):
    return jax.shard_map(
        shards,
        mesh=mesh,
        in_specs=(P("row", "col", None), P("col", "row"), P("col", "row"), P(), P("col", None)),
        out_specs=P("col", "row"),
        check_vma=False,
    )
```

```python
import jax
import jax.numpy as jnp
from jax import lax
from jax.experimental import pallas as pl
from jax.experimental.pallas import tpu as pltpu
from jax.sharding import PartitionSpec as P

NY, NZ, NC = 2, 8, 2
NROW = NY * NZ * NC
NH, NX = 2, 4
ND = 6
KW = 512
COLS = 256
PARTS = 2
CH = KW // NROW // PARTS
QUAD = NY * NC * CH
SPAN = NZ * QUAD
HALF = ND // 2


def chunk_of(zz, yy, cc):
    return (zz * NY + yy) * NC + cc


def row_of(zz, yy, cc):
    return (yy * NZ + zz) * NC + cc


def kernel(
    offsets_hbm,
    owners_hbm,
    left,
    right,
    out,
    offsets,
    owners,
    spread_first,
    spread_second,
    chosen,
    partner_chosen,
    gathered,
    rights,
    right_hi,
    right_lo,
    own_sum,
    send_par,
    recv_par,
    spread_send,
    spread_recv,
    swap_send,
    swap_recv,
    right_send,
    right_recv,
    local_sem,
    gather_send,
    gather_recv,
    par_send,
    par_recv,
):
    spread = (spread_first, spread_second)
    row = lax.axis_index("row")
    col = lax.axis_index("col")
    y = row // (NZ * NC)
    z = (row // NC) % NZ
    c = row % NC
    h = col // NX
    x = col % NX
    mine = chunk_of(z, y, c)
    east = h * NX + (x + 1) % NX
    west = h * NX + (x + NX - 1) % NX
    partner = (1 - h) * NX + x
    x_west = (x + NX - 1) % NX
    x_east = (x + 1) % NX
    x_far = (x + 2) % NX

    local_right = pltpu.make_async_copy(right, rights.at[x], local_sem.at[0])
    local_right.start()
    tables = []
    for number, (source, target) in enumerate(((offsets_hbm, offsets), (owners_hbm, owners))):
        copy = pltpu.make_async_copy(source, target, local_sem.at[1 + PARTS + number])
        copy.start()
        tables.append(copy)
    local_left = []
    for part in range(PARTS):
        begin = pl.multiple_of(part * SPAN + mine * CH, CH)
        copy = pltpu.make_async_copy(
            left.at[0, pl.ds(begin, CH)], spread[part].at[row], local_sem.at[1 + part]
        )
        copy.start()
        local_left.append(copy)

    barrier = pltpu.get_barrier_semaphore()

    def greet(step, carry):
        pl.semaphore_signal(barrier, inc=1, device_id={"row": (row + step) % NROW})
        return carry

    lax.fori_loop(1, NROW, greet, 0)
    for where in (east, west, partner):
        pl.semaphore_signal(barrier, inc=1, device_id={"col": where})
    pl.semaphore_wait(barrier, NROW - 1 + 3)

    def right_copy(source_ref, owner, slot, way, where):
        return pltpu.make_async_remote_copy(
            src_ref=source_ref,
            dst_ref=rights.at[owner, slot],
            send_sem=right_send.at[way, slot],
            recv_sem=right_recv.at[owner, slot],
            device_id={"col": where},
        )

    def right_wait(owner, slot):
        right_copy(rights.at[owner, slot], owner, slot, 0, east).wait_recv()

    first = []
    for slot_east, slot_west in ((0, 1), (1, 0)):
        for way, slot, where in ((0, slot_east, east), (1, slot_west, west)):
            copy = right_copy(right.at[slot], x, slot, way, where)
            first.append(copy)

    place = y * NZ + z

    def spread_to(part, spot, cc):
        yy = spot // NZ
        zz = spot % NZ
        begin = pl.multiple_of(part * SPAN + chunk_of(zz, yy, cc) * CH, CH)
        pltpu.make_async_remote_copy(
            src_ref=left.at[0, pl.ds(begin, CH)],
            dst_ref=spread[part].at[row],
            send_sem=spread_send.at[part],
            recv_sem=spread_recv.at[part],
            device_id={"row": row_of(zz, yy, cc)},
        ).start()

    def spread_stage(part, cc):
        def spread_start(step, carry):
            spread_to(part, (place + step) % (NY * NZ), cc)
            return carry

        lax.fori_loop(1, NY * NZ, spread_start, 0)

        @pl.when(c != cc)
        def _():
            spread_to(part, place, cc)

    def spread_all(part):
        ref = spread[part].at[pl.ds(0, NROW - 1)]
        return pltpu.make_async_remote_copy(
            src_ref=ref,
            dst_ref=ref,
            send_sem=spread_send.at[part],
            recv_sem=spread_recv.at[part],
            device_id={"col": partner},
        )

    def swap_copy(part):
        return pltpu.make_async_remote_copy(
            src_ref=chosen.at[part],
            dst_ref=partner_chosen.at[part],
            send_sem=swap_send.at[part],
            recv_sem=swap_recv.at[part],
            device_id={"col": partner},
        )

    def crossing(number):
        return ((x + offsets[number] // 2) // NX) % 2

    def choose_stage(part):
        local_left[part].wait()
        spread_all(part).wait_recv()
        for number in range(ND):
            chosen[part, number] = spread[part][owners[0, number]]
        swap_copy(part).start()

    beside = {"row": row_of(z, y, 1 - c)}
    across = {"row": row_of(z, 1 - y, c)}
    up = {"row": row_of((z + 1) % NZ, y, c)}
    down = {"row": row_of((z + NZ - 1) % NZ, y, c)}
    BESIDE, ACROSS, UP, DOWN = 0, 1, 2, 3
    targets = {BESIDE: beside, ACROSS: across, UP: up, DOWN: down}
    sent = [{way: 0 for way in targets} for part in range(PARTS)]

    def unit_copy(part, zz, yy, cc, half, way):
        chunk = chunk_of(zz, yy, cc)
        ref = gathered.at[part, chunk, pl.ds(half * HALF, HALF)]
        return pltpu.make_async_remote_copy(
            src_ref=ref,
            dst_ref=ref,
            send_sem=gather_send.at[part, way],
            recv_sem=gather_recv.at[part, chunk, half],
            device_id=targets[way],
        )

    def send(part, zz, yy, cc, half, *ways):
        for way in ways:
            sent[part][way] += 1
            unit_copy(part, zz, yy, cc, half, way).start()

    def receive(part, zz, yy, cc, half):
        unit_copy(part, zz, yy, cc, half, BESIDE).wait_recv()

    def open_stage(part):
        swap_copy(part).wait_recv()
        for number in range(ND):
            gathered[part, mine, number] = jnp.where(
                crossing(number) == 1, partner_chosen[part, number], chosen[part, number]
            )
        send(part, z, y, c, 0, ACROSS, UP, DOWN)
        send(part, z, y, c, 1, UP, DOWN, ACROSS)
        send(part, z, y, c, 0, BESIDE)
        send(part, z, y, c, 1, BESIDE)

    def passing(part, zz, yy, half, *ways):
        def go():
            receive(part, zz, yy, c, half)
            send(part, zz, yy, c, half, *ways)

        return go

    def neighbour_units(part):
        return [passing(part, z, 1 - y, 0, UP, DOWN, BESIDE)]

    def z_units(part, step):
        found = []
        below = (z + NZ - step) % NZ
        above = (z + step) % NZ
        far = step == NZ // 2
        last = step == NZ // 2 - 1
        units = ((y, 0), (y, 1), (1 - y, 0))
        if far:
            units += ((1 - y, 1),)
        for yy, half in units:
            extra = (ACROSS, BESIDE) if half == 1 and not far else (BESIDE,)
            if not (far and half == 1):
                on = () if far or (last and half == 1) else (UP,)
                found.append(passing(part, below, yy, half, *(on + extra)))
            if not (far and half == 0):
                on = () if far or (last and half == 0) else (DOWN,)
                found.append(passing(part, above, yy, half, *(on + extra)))
        return found

    def places(step):
        if step == 0:
            return (z,)
        if step == NZ // 2:
            return ((z + step) % NZ,)
        return ((z + NZ - step) % NZ, (z + step) % NZ)

    def y_units(part, step):
        found = []
        last = step == NZ // 2 - 1
        for number, zz in enumerate(places(step)):
            on = (DOWN,) if last and number == 1 else ()
            found.append(passing(part, zz, 1 - y, 1, *(on + (BESIDE,))))
        return found

    def prepare_right():
        local_right.wait()
        right_wait(x_west, 1)
        right_wait(x_east, 0)
        right_wait(x_far, 0)
        right_wait(x_far, 1)

        def prepare(number, carry):
            off = offsets[number]
            block = rights[(x + off // 2) % NX, off % 2]
            hi = block.astype(jnp.bfloat16)
            right_hi[number] = hi
            right_lo[number] = (block - hi.astype(jnp.float32)).astype(jnp.bfloat16)
            return carry

        lax.fori_loop(0, ND, prepare, 0)

    def par_copy(index, begin, rows):
        return pltpu.make_async_remote_copy(
            src_ref=send_par.at[pl.ds(begin, rows)],
            dst_ref=recv_par.at[pl.ds(begin, rows)],
            send_sem=par_send.at[index],
            recv_sem=par_recv.at[index],
            device_id={"col": partner},
        )

    def multiply(part, spots, begin, rows, numbers):
        if numbers[0] == 0:
            own_sum[pl.ds(begin, rows)] = jnp.zeros((rows, COLS), jnp.float32)
            send_par[pl.ds(begin, rows)] = jnp.zeros((rows, COLS), jnp.float32)

        def add_term(number, carry):
            pieces = [
                gathered[part, pl.ds(zz * NY * NC, NY * NC), number].reshape(QUAD, KW)
                for zz in spots
            ]
            block = jnp.concatenate(pieces, axis=0)
            hi = block.astype(jnp.bfloat16)
            lo = (block - hi.astype(jnp.float32)).astype(jnp.bfloat16)
            both = jnp.concatenate([hi, lo], axis=0)
            twice = jnp.dot(both, right_hi[number], preferred_element_type=jnp.float32)
            term = jnp.dot(hi, right_lo[number], preferred_element_type=jnp.float32)
            term += twice[:rows] + twice[rows:]
            zero = jnp.zeros_like(term)
            crossed = crossing(number) == 1
            own_sum[pl.ds(begin, rows)] += jnp.where(crossed, zero, term)
            send_par[pl.ds(begin, rows)] += jnp.where(crossed, term, zero)
            return carry

        lax.fori_loop(*numbers, add_term, 0)

    def wait_beside(part, spots):
        for zz in spots:
            for yy in (0, 1):
                for half in (0, 1):
                    receive(part, zz, yy, 1 - c, half)

    near = [spot for step in range(NZ // 2 - 1) for spot in places(step)]
    late = [spot for step in (NZ // 2 - 1, NZ // 2) for spot in places(step)]
    jobs = []
    for part in range(PARTS):
        for spots in (near, late):
            begin = jobs[-1][2] + jobs[-1][3] if jobs else 0
            jobs.append((part, spots, begin, len(spots) * QUAD))

    def multiply_units(job, slices=1):
        part, spots, begin, rows = jobs[job]
        size = ND // slices

        def piece(index):
            def go():
                if index == 0:
                    wait_beside(part, spots)
                multiply(part, spots, begin, rows, (index * size, index * size + size))
                if index == slices - 1:
                    par_copy(job, begin, rows).start()

            return go

        return [piece(index) for index in range(slices)]

    def run(*lists):
        longest = max(len(units) for units in lists)
        for turn in range(longest):
            for units in lists:
                first_unit = -(-turn * len(units) // longest)
                last_unit = -(-(turn + 1) * len(units) // longest)
                for unit in units[first_unit:last_unit]:
                    unit()

    def finish_stage(job):
        part, spots, begin, rows = jobs[job]
        par_copy(job, begin, rows).wait_recv()
        for number, zz in enumerate(spots):
            piece = pl.ds(begin + number * QUAD, QUAD)
            place = pl.multiple_of(part * SPAN + zz * QUAD, QUAD)
            out[pl.ds(place, QUAD)] = own_sum[piece] + recv_par[piece]

    spread_stage(0, 0)
    spread_stage(0, 1)
    for copy in first:
        copy.start()

    @pl.when(c == 1)
    def _():
        spread_stage(1, 0)

    for copy in tables:
        copy.wait()
    choose_stage(0)

    @pl.when(c == 0)
    def _():
        spread_stage(1, 0)

    spread_stage(1, 1)
    open_stage(0)
    run(neighbour_units(0))
    choose_stage(1)
    right_wait(x_west, 0)
    relay_east = right_copy(rights.at[x_west, 0], x_west, 0, 2, east)
    relay_east.start()
    right_wait(x_east, 1)
    relay_west = right_copy(rights.at[x_east, 1], x_east, 1, 2, west)
    relay_west.start()
    run(z_units(0, 1), y_units(0, 0))
    run(z_units(0, 2))
    open_stage(1)
    run(y_units(0, 1))
    run(z_units(0, 3), neighbour_units(1))
    run(y_units(0, 2))
    run(z_units(1, 1), y_units(1, 0))
    run(y_units(0, 3))
    run(z_units(1, 2), z_units(0, 4))
    run(y_units(1, 1))
    prepare_right()
    run(z_units(1, 3), multiply_units(0, 3))
    run(y_units(1, 2))
    run(y_units(1, 3), multiply_units(1, 3))
    run(multiply_units(2))
    run(z_units(1, 4))
    run(multiply_units(3))
    for job in range(len(jobs)):
        finish_stage(job)

    for copy in first + [relay_east, relay_west]:
        copy.wait_send()
    for part in range(PARTS):
        spread_all(part).wait_send()
        swap_copy(part).wait_send()
        for way in targets:
            ref = gathered.at[part, pl.ds(0, sent[part][way]), pl.ds(0, HALF)]
            pltpu.make_async_remote_copy(
                src_ref=ref,
                dst_ref=ref,
                send_sem=gather_send.at[part, way],
                recv_sem=gather_recv.at[part, 0, 0],
                device_id=targets[way],
            ).wait_send()
    for index, (part, spots, begin, rows) in enumerate(jobs):
        par_copy(index, begin, rows).wait_send()


def shards(left_slots, right, previous, offsets, owners):
    f32 = jnp.float32
    vmem = pl.BlockSpec(memory_space=pltpu.VMEM)
    hbm = pl.BlockSpec(memory_space=pltpu.HBM)
    dma = pltpu.SemaphoreType.DMA
    operands = (offsets, owners, left_slots, right.reshape(2, KW, COLS))
    total = pl.pallas_call(
        kernel,
        out_shape=jax.ShapeDtypeStruct((KW, COLS), f32),
        in_specs=[hbm] * 4,
        out_specs=vmem,
        scratch_shapes=[
            pltpu.SMEM((ND,), jnp.int32),
            pltpu.SMEM((1, ND), jnp.int32),
            pltpu.VMEM((NROW, CH, KW), f32),
            pltpu.VMEM((NROW, CH, KW), f32),
            pltpu.VMEM((PARTS, ND, CH, KW), f32),
            pltpu.VMEM((PARTS, ND, CH, KW), f32),
            pltpu.VMEM((PARTS, NROW, ND, CH, KW), f32),
            pltpu.VMEM((NX, 2, KW, COLS), f32),
            pltpu.VMEM((ND, KW, COLS), jnp.bfloat16),
            pltpu.VMEM((ND, KW, COLS), jnp.bfloat16),
            pltpu.VMEM((KW, COLS), f32),
            pltpu.VMEM((KW, COLS), f32),
            pltpu.VMEM((KW, COLS), f32),
            dma((PARTS,)),
            dma((PARTS,)),
            dma((PARTS,)),
            dma((PARTS,)),
            dma((3, 2)),
            dma((NX, 2)),
            dma((3 + PARTS,)),
            dma((PARTS, 4)),
            dma((PARTS, NROW, 2)),
            dma((4,)),
            dma((4,)),
        ],
        compiler_params=pltpu.CompilerParams(
            collective_id=0, has_side_effects=True, vmem_limit_bytes=48 * 1024 * 1024
        ),
    )(*(pltpu.with_memory_space_constraint(a, pltpu.HBM) for a in operands))
    return 2.0 * previous - total


def solution(mesh):
    return jax.shard_map(
        shards,
        mesh=mesh,
        in_specs=(P("row", "col", None), P("col", "row"), P("col", "row"), P(), P("col", None)),
        out_specs=P("col", "row"),
        check_vma=False,
    )
```

```python
import jax
import jax.numpy as jnp
from jax import lax
from jax.experimental import pallas as pl
from jax.experimental.pallas import tpu as pltpu
from jax.sharding import PartitionSpec as P

NY, NZ, NC = 2, 8, 2
NROW = NY * NZ * NC
NH, NX = 2, 4
ND = 6
KW = 512
COLS = 256
PARTS = 2
CH = KW // NROW // PARTS
TURN = (3, 1)
QUAD = NY * NC * CH
SPAN = NZ * QUAD
HALF = ND // 2


def chunk_of(zz, yy, cc):
    return (zz * NY + yy) * NC + cc


def row_of(zz, yy, cc):
    return (yy * NZ + zz) * NC + cc


def kernel(
    offsets_hbm,
    owners_hbm,
    left,
    right,
    out,
    offsets,
    owners,
    spread_first,
    spread_second,
    chosen,
    partner_chosen,
    gathered,
    rights,
    right_hi,
    right_lo,
    own_sum,
    send_par,
    recv_par,
    spread_send,
    spread_recv,
    swap_send,
    swap_recv,
    right_send,
    right_recv,
    local_sem,
    gather_send,
    gather_recv,
    par_send,
    par_recv,
):
    spread = (spread_first, spread_second)
    row = lax.axis_index("row")
    col = lax.axis_index("col")
    y = row // (NZ * NC)
    z = (row // NC) % NZ
    c = row % NC
    h = col // NX
    x = col % NX
    mine = chunk_of(z, y, c)
    east = h * NX + (x + 1) % NX
    west = h * NX + (x + NX - 1) % NX
    partner = (1 - h) * NX + x
    x_west = (x + NX - 1) % NX
    x_east = (x + 1) % NX
    x_far = (x + 2) % NX

    local_right = pltpu.make_async_copy(right, rights.at[x], local_sem.at[0])
    local_right.start()
    tables = []
    for number, (source, target) in enumerate(((offsets_hbm, offsets), (owners_hbm, owners))):
        copy = pltpu.make_async_copy(source, target, local_sem.at[1 + PARTS + number])
        copy.start()
        tables.append(copy)
    local_left = []
    for part in range(PARTS):
        begin = pl.multiple_of(part * SPAN + mine * CH, CH)
        copy = pltpu.make_async_copy(
            left.at[0, pl.ds(begin, CH)], spread[part].at[row], local_sem.at[1 + part]
        )
        copy.start()
        local_left.append(copy)

    barrier = pltpu.get_barrier_semaphore()

    def greet(step, carry):
        pl.semaphore_signal(barrier, inc=1, device_id={"row": (row + step) % NROW})
        return carry

    lax.fori_loop(1, NROW, greet, 0)
    for where in (east, west, partner):
        pl.semaphore_signal(barrier, inc=1, device_id={"col": where})
    pl.semaphore_wait(barrier, NROW - 1 + 3)

    def right_copy(source_ref, owner, slot, way, where):
        return pltpu.make_async_remote_copy(
            src_ref=source_ref,
            dst_ref=rights.at[owner, slot],
            send_sem=right_send.at[way, slot],
            recv_sem=right_recv.at[owner, slot],
            device_id={"col": where},
        )

    def right_wait(owner, slot):
        right_copy(rights.at[owner, slot], owner, slot, 0, east).wait_recv()

    first = []
    for slot_east, slot_west in ((0, 1), (1, 0)):
        for way, slot, where in ((0, slot_east, east), (1, slot_west, west)):
            copy = right_copy(right.at[slot], x, slot, way, where)
            first.append(copy)

    place = y * NZ + z

    def spread_to(part, spot, cc):
        yy = spot // NZ
        zz = spot % NZ
        begin = pl.multiple_of(part * SPAN + chunk_of(zz, yy, cc) * CH, CH)
        pltpu.make_async_remote_copy(
            src_ref=left.at[0, pl.ds(begin, CH)],
            dst_ref=spread[part].at[row],
            send_sem=spread_send.at[part],
            recv_sem=spread_recv.at[part],
            device_id={"row": row_of(zz, yy, cc)},
        ).start()

    def spread_stage(part, cc):
        def spread_start(step, carry):
            spread_to(part, (place + step) % (NY * NZ), cc)
            return carry

        lax.fori_loop(1, NY * NZ, spread_start, 0)

        @pl.when(c != cc)
        def _():
            spread_to(part, place, cc)

    def spread_all(part):
        ref = spread[part].at[pl.ds(0, NROW - 1)]
        return pltpu.make_async_remote_copy(
            src_ref=ref,
            dst_ref=ref,
            send_sem=spread_send.at[part],
            recv_sem=spread_recv.at[part],
            device_id={"col": partner},
        )

    def swap_copy(part, half):
        piece = pl.ds(half * HALF, HALF)
        return pltpu.make_async_remote_copy(
            src_ref=chosen.at[part, piece],
            dst_ref=partner_chosen.at[part, piece],
            send_sem=swap_send.at[part, half],
            recv_sem=swap_recv.at[part, half],
            device_id={"col": partner},
        )

    def crossing(number):
        return ((x + offsets[number] // 2) // NX) % 2

    def choose_stage(part):
        local_left[part].wait()
        spread_all(part).wait_recv()
        for half in (0, 1):
            for number in range(half * HALF, half * HALF + HALF):
                chosen[part, number] = spread[part][owners[0, number]]
            swap_copy(part, half).start()

    beside = {"row": row_of(z, y, 1 - c)}
    across = {"row": row_of(z, 1 - y, c)}
    up = {"row": row_of((z + 1) % NZ, y, c)}
    down = {"row": row_of((z + NZ - 1) % NZ, y, c)}
    BESIDE, ACROSS, UP, DOWN = 0, 1, 2, 3
    targets = {BESIDE: beside, ACROSS: across, UP: up, DOWN: down}
    sent = [{way: 0 for way in targets} for part in range(PARTS)]

    def unit_copy(part, zz, yy, cc, half, way):
        chunk = chunk_of(zz, yy, cc)
        ref = gathered.at[part, chunk, pl.ds(half * HALF, HALF)]
        return pltpu.make_async_remote_copy(
            src_ref=ref,
            dst_ref=ref,
            send_sem=gather_send.at[part, way],
            recv_sem=gather_recv.at[part, chunk, half],
            device_id=targets[way],
        )

    def send(part, zz, yy, cc, half, *ways):
        for way in ways:
            sent[part][way] += 1
            unit_copy(part, zz, yy, cc, half, way).start()

    def receive(part, zz, yy, cc, half):
        unit_copy(part, zz, yy, cc, half, BESIDE).wait_recv()

    def open_units(part):
        def opening(half, *ways):
            def go():
                swap_copy(part, half).wait_recv()
                for number in range(half * HALF, half * HALF + HALF):
                    gathered[part, mine, number] = jnp.where(
                        crossing(number) == 1, partner_chosen[part, number], chosen[part, number]
                    )
                send(part, z, y, c, half, *ways)

            return go

        return [
            opening(0, ACROSS, UP, DOWN, BESIDE),
            opening(1, UP, DOWN, ACROSS, BESIDE),
        ]

    def passing(part, zz, yy, half, *ways):
        def go():
            receive(part, zz, yy, c, half)
            send(part, zz, yy, c, half, *ways)

        return go

    def neighbour_units(part):
        return [passing(part, z, 1 - y, 0, UP, DOWN, BESIDE)]

    def z_units(part, step):
        found = []
        below = (z + NZ - step) % NZ
        above = (z + step) % NZ
        far = step == NZ // 2
        last = step == NZ // 2 - 1
        early = step <= TURN[part]
        units = ((y, 0), (y, 1), (1 - y, 0))
        if not early:
            units += ((1 - y, 1),)
        for yy, half in units:
            extra = (ACROSS, BESIDE) if half == 1 and early else (BESIDE,)
            if not (far and half == 1):
                on = () if far or (last and half == 1) else (UP,)
                found.append(passing(part, below, yy, half, *(on + extra)))
            if not (far and half == 0):
                on = () if far or (last and half == 0) else (DOWN,)
                found.append(passing(part, above, yy, half, *(on + extra)))
        return found

    def places(step):
        if step == 0:
            return (z,)
        if step == NZ // 2:
            return ((z + step) % NZ,)
        return ((z + NZ - step) % NZ, (z + step) % NZ)

    def y_units(part, step):
        found = []
        if step > TURN[part]:
            return found
        for number, zz in enumerate(places(step)):
            on = ()
            if step == TURN[part]:
                if step == 0:
                    on = (UP, DOWN)
                elif number == 1:
                    on = (DOWN,)
                elif step < NZ // 2 - 1:
                    on = (UP,)
            found.append(passing(part, zz, 1 - y, 1, *(on + (BESIDE,))))
        return found

    def prepare_right():
        local_right.wait()
        right_wait(x_west, 1)
        right_wait(x_east, 0)
        right_wait(x_far, 0)
        right_wait(x_far, 1)

        def prepare(number, carry):
            off = offsets[number]
            block = rights[(x + off // 2) % NX, off % 2]
            hi = block.astype(jnp.bfloat16)
            right_hi[number] = hi
            right_lo[number] = (block - hi.astype(jnp.float32)).astype(jnp.bfloat16)
            return carry

        lax.fori_loop(0, ND, prepare, 0)

    def par_copy(index, begin, rows):
        return pltpu.make_async_remote_copy(
            src_ref=send_par.at[pl.ds(begin, rows)],
            dst_ref=recv_par.at[pl.ds(begin, rows)],
            send_sem=par_send.at[index],
            recv_sem=par_recv.at[index],
            device_id={"col": partner},
        )

    def multiply(part, spots, begin, rows, numbers):
        if numbers[0] == 0:
            own_sum[pl.ds(begin, rows)] = jnp.zeros((rows, COLS), jnp.float32)
            send_par[pl.ds(begin, rows)] = jnp.zeros((rows, COLS), jnp.float32)

        def add_term(number, carry):
            pieces = [
                gathered[part, pl.ds(zz * NY * NC, NY * NC), number].reshape(QUAD, KW)
                for zz in spots
            ]
            block = jnp.concatenate(pieces, axis=0)
            hi = block.astype(jnp.bfloat16)
            lo = (block - hi.astype(jnp.float32)).astype(jnp.bfloat16)
            both = jnp.concatenate([hi, lo], axis=0)
            twice = jnp.dot(both, right_hi[number], preferred_element_type=jnp.float32)
            term = jnp.dot(hi, right_lo[number], preferred_element_type=jnp.float32)
            term += twice[:rows] + twice[rows:]
            zero = jnp.zeros_like(term)
            crossed = crossing(number) == 1
            own_sum[pl.ds(begin, rows)] += jnp.where(crossed, zero, term)
            send_par[pl.ds(begin, rows)] += jnp.where(crossed, term, zero)
            return carry

        lax.fori_loop(*numbers, add_term, 0)

    def wait_beside(part, spots):
        for zz in spots:
            for yy in (0, 1):
                for half in (0, 1):
                    receive(part, zz, yy, 1 - c, half)

    def spots_of(*steps):
        return [spot for step in steps for spot in places(step)]

    jobs = []
    for part, steps in ((0, (0, 1, 2)), (0, (3, 4)), (1, (0, 1)), (1, (2, 3)), (1, (4,))):
        begin = jobs[-1][2] + jobs[-1][3] if jobs else 0
        spots = spots_of(*steps)
        jobs.append((part, spots, begin, len(spots) * QUAD))

    def multiply_units(job, slices=1):
        part, spots, begin, rows = jobs[job]
        size = ND // slices

        def piece(index):
            def go():
                if index == 0:
                    wait_beside(part, spots)
                multiply(part, spots, begin, rows, (index * size, index * size + size))
                if index == slices - 1:
                    par_copy(job, begin, rows).start()

            return go

        return [piece(index) for index in range(slices)]

    def by_core(zero, one):
        before = [dict(counts) for counts in sent]

        @pl.when(c == 0)
        def _():
            zero()

        for counts, saved in zip(sent, before):
            counts.update(saved)

        @pl.when(c == 1)
        def _():
            one()

    def run(*lists):
        longest = max(len(units) for units in lists)
        for turn in range(longest):
            for units in lists:
                first_unit = -(-turn * len(units) // longest)
                last_unit = -(-(turn + 1) * len(units) // longest)
                for unit in units[first_unit:last_unit]:
                    unit()

    def finish_stage(job):
        part, spots, begin, rows = jobs[job]
        par_copy(job, begin, rows).wait_recv()
        for number, zz in enumerate(spots):
            piece = pl.ds(begin + number * QUAD, QUAD)
            place = pl.multiple_of(part * SPAN + zz * QUAD, QUAD)
            out[pl.ds(place, QUAD)] = own_sum[piece] + recv_par[piece]

    spread_stage(0, 0)
    spread_stage(0, 1)
    for copy in first:
        copy.start()

    @pl.when(c == 1)
    def _():
        spread_stage(1, 0)

    for copy in tables:
        copy.wait()
    choose_stage(0)

    @pl.when(c == 0)
    def _():
        spread_stage(1, 0)

    spread_stage(1, 1)
    run(open_units(0))
    run(neighbour_units(0))
    choose_stage(1)
    right_wait(x_west, 0)
    relay_east = right_copy(rights.at[x_west, 0], x_west, 0, 2, east)
    relay_east.start()
    right_wait(x_east, 1)
    relay_west = right_copy(rights.at[x_east, 1], x_east, 1, 2, west)
    relay_west.start()
    def zero():
        run(open_units(1))
        run(z_units(0, 1), y_units(0, 0))

    def one():
        run(z_units(0, 1), y_units(0, 0))
        run(open_units(1))

    by_core(zero, one)
    run(y_units(0, 1))
    run(z_units(0, 2))
    run(neighbour_units(1))
    run(y_units(0, 2))
    run(y_units(1, 0))
    run(z_units(0, 3), z_units(1, 1))
    run(y_units(0, 3))
    run(y_units(1, 1))
    prepare_right()
    run(multiply_units(0, 3), z_units(1, 2))
    run(z_units(0, 4), multiply_units(2, 3))
    run(z_units(1, 3), multiply_units(1, 3))
    run(multiply_units(3, 3), z_units(1, 4))
    run(multiply_units(4))
    for job in range(len(jobs)):
        finish_stage(job)

    for copy in first + [relay_east, relay_west]:
        copy.wait_send()
    for part in range(PARTS):
        spread_all(part).wait_send()
        for half in (0, 1):
            swap_copy(part, half).wait_send()
        for way in targets:
            ref = gathered.at[part, pl.ds(0, sent[part][way]), pl.ds(0, HALF)]
            pltpu.make_async_remote_copy(
                src_ref=ref,
                dst_ref=ref,
                send_sem=gather_send.at[part, way],
                recv_sem=gather_recv.at[part, 0, 0],
                device_id=targets[way],
            ).wait_send()
    for index, (part, spots, begin, rows) in enumerate(jobs):
        par_copy(index, begin, rows).wait_send()


def shards(left_slots, right, previous, offsets, owners):
    f32 = jnp.float32
    vmem = pl.BlockSpec(memory_space=pltpu.VMEM)
    hbm = pl.BlockSpec(memory_space=pltpu.HBM)
    dma = pltpu.SemaphoreType.DMA
    operands = (offsets, owners, left_slots, right.reshape(2, KW, COLS))
    total = pl.pallas_call(
        kernel,
        out_shape=jax.ShapeDtypeStruct((KW, COLS), f32),
        in_specs=[hbm] * 4,
        out_specs=vmem,
        scratch_shapes=[
            pltpu.SMEM((ND,), jnp.int32),
            pltpu.SMEM((1, ND), jnp.int32),
            pltpu.VMEM((NROW, CH, KW), f32),
            pltpu.VMEM((NROW, CH, KW), f32),
            pltpu.VMEM((PARTS, ND, CH, KW), f32),
            pltpu.VMEM((PARTS, ND, CH, KW), f32),
            pltpu.VMEM((PARTS, NROW, ND, CH, KW), f32),
            pltpu.VMEM((NX, 2, KW, COLS), f32),
            pltpu.VMEM((ND, KW, COLS), jnp.bfloat16),
            pltpu.VMEM((ND, KW, COLS), jnp.bfloat16),
            pltpu.VMEM((KW, COLS), f32),
            pltpu.VMEM((KW, COLS), f32),
            pltpu.VMEM((KW, COLS), f32),
            dma((PARTS,)),
            dma((PARTS,)),
            dma((PARTS, 2)),
            dma((PARTS, 2)),
            dma((3, 2)),
            dma((NX, 2)),
            dma((3 + PARTS,)),
            dma((PARTS, 4)),
            dma((PARTS, NROW, 2)),
            dma((5,)),
            dma((5,)),
        ],
        compiler_params=pltpu.CompilerParams(
            collective_id=0, has_side_effects=True, vmem_limit_bytes=48 * 1024 * 1024
        ),
    )(*(pltpu.with_memory_space_constraint(a, pltpu.HBM) for a in operands))
    return 2.0 * previous - total


def solution(mesh):
    return jax.shard_map(
        shards,
        mesh=mesh,
        in_specs=(P("row", "col", None), P("col", "row"), P("col", "row"), P(), P("col", None)),
        out_specs=P("col", "row"),
        check_vma=False,
    )
```

```python
import jax
import jax.numpy as jnp
from jax import lax
from jax.experimental import pallas as pl
from jax.experimental.pallas import tpu as pltpu
from jax.sharding import PartitionSpec as P

NY, NZ, NC = 2, 8, 2
NROW = NY * NZ * NC
NH, NX = 2, 4
ND = 6
KW = 512
COLS = 256
PARTS = 2
CH = KW // NROW // PARTS
TURN = (3, 1)
QUAD = NY * NC * CH
SPAN = NZ * QUAD
HALF = ND // 2


def chunk_of(zz, yy, cc):
    return (zz * NY + yy) * NC + cc


def row_of(zz, yy, cc):
    return (yy * NZ + zz) * NC + cc


def kernel(
    offsets_hbm,
    owners_hbm,
    left,
    right,
    out,
    offsets,
    owners,
    spread_first,
    spread_second,
    chosen,
    partner_chosen,
    gathered,
    rights,
    right_hi,
    right_lo,
    own_sum,
    send_par,
    recv_par,
    spread_send,
    spread_recv,
    swap_send,
    swap_recv,
    right_send,
    right_recv,
    local_sem,
    gather_send,
    gather_recv,
    par_send,
    par_recv,
):
    spread = (spread_first, spread_second)
    row = lax.axis_index("row")
    col = lax.axis_index("col")
    y = row // (NZ * NC)
    z = (row // NC) % NZ
    c = row % NC
    h = col // NX
    x = col % NX
    mine = chunk_of(z, y, c)
    east = h * NX + (x + 1) % NX
    west = h * NX + (x + NX - 1) % NX
    partner = (1 - h) * NX + x
    x_west = (x + NX - 1) % NX
    x_east = (x + 1) % NX
    x_far = (x + 2) % NX

    local_right = pltpu.make_async_copy(right, rights.at[x], local_sem.at[0])
    local_right.start()
    tables = []
    for number, (source, target) in enumerate(((offsets_hbm, offsets), (owners_hbm, owners))):
        copy = pltpu.make_async_copy(source, target, local_sem.at[1 + PARTS + number])
        copy.start()
        tables.append(copy)
    local_left = []
    for part in range(PARTS):
        begin = pl.multiple_of(part * SPAN + mine * CH, CH)
        copy = pltpu.make_async_copy(
            left.at[0, pl.ds(begin, CH)], spread[part].at[row], local_sem.at[1 + part]
        )
        copy.start()
        local_left.append(copy)

    barrier = pltpu.get_barrier_semaphore()

    def greet(step, carry):
        pl.semaphore_signal(barrier, inc=1, device_id={"row": (row + step) % NROW})
        return carry

    lax.fori_loop(1, NROW, greet, 0)
    for where in (east, west, partner):
        pl.semaphore_signal(barrier, inc=1, device_id={"col": where})
    pl.semaphore_wait(barrier, NROW - 1 + 3)

    def right_copy(source_ref, owner, slot, way, where):
        return pltpu.make_async_remote_copy(
            src_ref=source_ref,
            dst_ref=rights.at[owner, slot],
            send_sem=right_send.at[way, slot],
            recv_sem=right_recv.at[owner, slot],
            device_id={"col": where},
        )

    def right_wait(owner, slot):
        right_copy(rights.at[owner, slot], owner, slot, 0, east).wait_recv()

    first = []
    for slot_east, slot_west in ((0, 1), (1, 0)):
        for way, slot, where in ((0, slot_east, east), (1, slot_west, west)):
            copy = right_copy(right.at[slot], x, slot, way, where)
            first.append(copy)

    place = y * NZ + z

    def spread_to(part, spot, cc):
        yy = spot // NZ
        zz = spot % NZ
        begin = pl.multiple_of(part * SPAN + chunk_of(zz, yy, cc) * CH, CH)
        pltpu.make_async_remote_copy(
            src_ref=left.at[0, pl.ds(begin, CH)],
            dst_ref=spread[part].at[row],
            send_sem=spread_send.at[part],
            recv_sem=spread_recv.at[part],
            device_id={"row": row_of(zz, yy, cc)},
        ).start()

    def spread_stage(part, cc):
        def spread_start(step, carry):
            spread_to(part, (place + step) % (NY * NZ), cc)
            return carry

        lax.fori_loop(1, NY * NZ, spread_start, 0)

        @pl.when(c != cc)
        def _():
            spread_to(part, place, cc)

    def spread_all(part):
        ref = spread[part].at[pl.ds(0, NROW - 1)]
        return pltpu.make_async_remote_copy(
            src_ref=ref,
            dst_ref=ref,
            send_sem=spread_send.at[part],
            recv_sem=spread_recv.at[part],
            device_id={"col": partner},
        )

    def swap_copy(part, half):
        piece = pl.ds(half * HALF, HALF)
        return pltpu.make_async_remote_copy(
            src_ref=chosen.at[part, piece],
            dst_ref=partner_chosen.at[part, piece],
            send_sem=swap_send.at[part, half],
            recv_sem=swap_recv.at[part, half],
            device_id={"col": partner},
        )

    def crossing(number):
        return ((x + offsets[number] // 2) // NX) % 2

    def choose_stage(part):
        local_left[part].wait()
        spread_all(part).wait_recv()
        for half in (0, 1):
            for number in range(half * HALF, half * HALF + HALF):
                chosen[part, number] = spread[part][owners[0, number]]
            swap_copy(part, half).start()

    beside = {"row": row_of(z, y, 1 - c)}
    across = {"row": row_of(z, 1 - y, c)}
    up = {"row": row_of((z + 1) % NZ, y, c)}
    down = {"row": row_of((z + NZ - 1) % NZ, y, c)}
    BESIDE, ACROSS, UP, DOWN = 0, 1, 2, 3
    targets = {BESIDE: beside, ACROSS: across, UP: up, DOWN: down}
    sent = [{way: 0 for way in targets} for part in range(PARTS)]

    def unit_copy(part, zz, yy, cc, half, way):
        chunk = chunk_of(zz, yy, cc)
        ref = gathered.at[part, chunk, pl.ds(half * HALF, HALF)]
        return pltpu.make_async_remote_copy(
            src_ref=ref,
            dst_ref=ref,
            send_sem=gather_send.at[part, way],
            recv_sem=gather_recv.at[part, chunk, half],
            device_id=targets[way],
        )

    def send(part, zz, yy, cc, half, *ways):
        for way in ways:
            sent[part][way] += 1
            unit_copy(part, zz, yy, cc, half, way).start()

    def receive(part, zz, yy, cc, half):
        unit_copy(part, zz, yy, cc, half, BESIDE).wait_recv()

    def open_units(part):
        def opening(half, *ways):
            def go():
                swap_copy(part, half).wait_recv()
                for number in range(half * HALF, half * HALF + HALF):
                    gathered[part, mine, number] = jnp.where(
                        crossing(number) == 1, partner_chosen[part, number], chosen[part, number]
                    )
                send(part, z, y, c, half, *ways)

            return go

        return [
            opening(0, ACROSS, UP, DOWN, BESIDE),
            opening(1, UP, DOWN, ACROSS, BESIDE),
        ]

    def passing(part, zz, yy, half, *ways):
        def go():
            receive(part, zz, yy, c, half)
            send(part, zz, yy, c, half, *ways)

        return go

    def neighbour_units(part):
        return [passing(part, z, 1 - y, 0, UP, DOWN, BESIDE)]

    def z_units(part, step):
        found = []
        below = (z + NZ - step) % NZ
        above = (z + step) % NZ
        far = step == NZ // 2
        last = step == NZ // 2 - 1
        early = step <= TURN[part]
        units = ((y, 0), (y, 1), (1 - y, 0))
        if not early:
            units += ((1 - y, 1),)
        for yy, half in units:
            extra = (ACROSS, BESIDE) if half == 1 and early else (BESIDE,)
            if not (far and half == 1):
                on = () if far or (last and half == 1) else (UP,)
                found.append(passing(part, below, yy, half, *(on + extra)))
            if not (far and half == 0):
                on = () if far or (last and half == 0) else (DOWN,)
                found.append(passing(part, above, yy, half, *(on + extra)))
        return found

    def places(step):
        if step == 0:
            return (z,)
        if step == NZ // 2:
            return ((z + step) % NZ,)
        return ((z + NZ - step) % NZ, (z + step) % NZ)

    def y_units(part, step):
        found = []
        if step > TURN[part]:
            return found
        for number, zz in enumerate(places(step)):
            on = ()
            if step == TURN[part]:
                if step == 0:
                    on = (UP, DOWN)
                elif number == 1:
                    on = (DOWN,)
                elif step < NZ // 2 - 1:
                    on = (UP,)
            found.append(passing(part, zz, 1 - y, 1, *(on + (BESIDE,))))
        return found

    def prepare_right():
        local_right.wait()
        right_wait(x_west, 1)
        right_wait(x_east, 0)
        right_wait(x_far, 0)
        right_wait(x_far, 1)

        def prepare(number, carry):
            off = offsets[number]
            block = rights[(x + off // 2) % NX, off % 2]
            hi = block.astype(jnp.bfloat16)
            right_hi[number] = hi
            right_lo[number] = (block - hi.astype(jnp.float32)).astype(jnp.bfloat16)
            return carry

        lax.fori_loop(0, ND, prepare, 0)

    def par_copy(index, begin, rows):
        return pltpu.make_async_remote_copy(
            src_ref=send_par.at[pl.ds(begin, rows)],
            dst_ref=recv_par.at[pl.ds(begin, rows)],
            send_sem=par_send.at[index],
            recv_sem=par_recv.at[index],
            device_id={"col": partner},
        )

    def multiply(part, spots, begin, rows, numbers):
        if numbers[0] == 0:
            own_sum[pl.ds(begin, rows)] = jnp.zeros((rows, COLS), jnp.float32)
            send_par[pl.ds(begin, rows)] = jnp.zeros((rows, COLS), jnp.float32)

        def add_term(number, carry):
            pieces = [
                gathered[part, pl.ds(zz * NY * NC, NY * NC), number].reshape(QUAD, KW)
                for zz in spots
            ]
            block = jnp.concatenate(pieces, axis=0)
            hi = block.astype(jnp.bfloat16)
            lo = (block - hi.astype(jnp.float32)).astype(jnp.bfloat16)
            both = jnp.concatenate([hi, lo], axis=0)
            twice = jnp.dot(both, right_hi[number], preferred_element_type=jnp.float32)
            term = jnp.dot(hi, right_lo[number], preferred_element_type=jnp.float32)
            term += twice[:rows] + twice[rows:]
            zero = jnp.zeros_like(term)
            crossed = crossing(number) == 1
            own_sum[pl.ds(begin, rows)] += jnp.where(crossed, zero, term)
            send_par[pl.ds(begin, rows)] += jnp.where(crossed, term, zero)
            return carry

        lax.fori_loop(*numbers, add_term, 0)

    def wait_beside(part, spots):
        for zz in spots:
            for yy in (0, 1):
                for half in (0, 1):
                    receive(part, zz, yy, 1 - c, half)

    def spots_of(*steps):
        return [spot for step in steps for spot in places(step)]

    jobs = []
    for part, steps in ((0, (0, 1, 2)), (0, (3, 4)), (1, (0, 1)), (1, (2, 3)), (1, (4,))):
        begin = jobs[-1][2] + jobs[-1][3] if jobs else 0
        spots = spots_of(*steps)
        jobs.append((part, spots, begin, len(spots) * QUAD))

    def multiply_units(job, slices=1):
        part, spots, begin, rows = jobs[job]
        size = ND // slices

        def piece(index):
            def go():
                if index == 0:
                    wait_beside(part, spots)
                multiply(part, spots, begin, rows, (index * size, index * size + size))
                if index == slices - 1:
                    par_copy(job, begin, rows).start()

            return go

        return [piece(index) for index in range(slices)]

    def by_core(zero, one):
        before = [dict(counts) for counts in sent]

        @pl.when(c == 0)
        def _():
            zero()

        for counts, saved in zip(sent, before):
            counts.update(saved)

        @pl.when(c == 1)
        def _():
            one()

    def run(*lists):
        longest = max(len(units) for units in lists)
        for turn in range(longest):
            for units in lists:
                first_unit = -(-turn * len(units) // longest)
                last_unit = -(-(turn + 1) * len(units) // longest)
                for unit in units[first_unit:last_unit]:
                    unit()

    def finish_stage(job):
        part, spots, begin, rows = jobs[job]
        par_copy(job, begin, rows).wait_recv()
        for number, zz in enumerate(spots):
            piece = pl.ds(begin + number * QUAD, QUAD)
            place = pl.multiple_of(part * SPAN + zz * QUAD, QUAD)
            out[pl.ds(place, QUAD)] = own_sum[piece] + recv_par[piece]

    spread_stage(0, 0)
    spread_stage(0, 1)
    for copy in first:
        copy.start()

    @pl.when(c == 1)
    def _():
        spread_stage(1, 0)

    for copy in tables:
        copy.wait()
    choose_stage(0)

    @pl.when(c == 0)
    def _():
        spread_stage(1, 0)

    spread_stage(1, 1)
    run(open_units(0))
    run(neighbour_units(0))
    choose_stage(1)
    right_wait(x_west, 0)
    relay_east = right_copy(rights.at[x_west, 0], x_west, 0, 2, east)
    relay_east.start()
    right_wait(x_east, 1)
    relay_west = right_copy(rights.at[x_east, 1], x_east, 1, 2, west)
    relay_west.start()
    def zero():
        run(open_units(1))
        run(z_units(0, 1), y_units(0, 0))

    def one():
        run(z_units(0, 1), y_units(0, 0))
        run(open_units(1))

    by_core(zero, one)
    run(z_units(0, 2), y_units(0, 1))
    run(neighbour_units(1))
    run(y_units(0, 2))
    run(z_units(0, 3), z_units(1, 1), y_units(1, 0))
    run(y_units(1, 1), y_units(0, 3))
    prepare_right()
    run(multiply_units(0, 3), z_units(1, 2))
    run(z_units(0, 4), multiply_units(2, 3))
    run(z_units(1, 3), multiply_units(1, 3))
    run(multiply_units(3, 3), z_units(1, 4))
    run(multiply_units(4))
    for job in range(len(jobs)):
        finish_stage(job)

    for copy in first + [relay_east, relay_west]:
        copy.wait_send()
    for part in range(PARTS):
        spread_all(part).wait_send()
        for half in (0, 1):
            swap_copy(part, half).wait_send()
        for way in targets:
            ref = gathered.at[part, pl.ds(0, sent[part][way]), pl.ds(0, HALF)]
            pltpu.make_async_remote_copy(
                src_ref=ref,
                dst_ref=ref,
                send_sem=gather_send.at[part, way],
                recv_sem=gather_recv.at[part, 0, 0],
                device_id=targets[way],
            ).wait_send()
    for index, (part, spots, begin, rows) in enumerate(jobs):
        par_copy(index, begin, rows).wait_send()


def shards(left_slots, right, previous, offsets, owners):
    f32 = jnp.float32
    vmem = pl.BlockSpec(memory_space=pltpu.VMEM)
    hbm = pl.BlockSpec(memory_space=pltpu.HBM)
    dma = pltpu.SemaphoreType.DMA
    operands = (offsets, owners, left_slots, right.reshape(2, KW, COLS))
    total = pl.pallas_call(
        kernel,
        out_shape=jax.ShapeDtypeStruct((KW, COLS), f32),
        in_specs=[hbm] * 4,
        out_specs=vmem,
        scratch_shapes=[
            pltpu.SMEM((ND,), jnp.int32),
            pltpu.SMEM((1, ND), jnp.int32),
            pltpu.VMEM((NROW, CH, KW), f32),
            pltpu.VMEM((NROW, CH, KW), f32),
            pltpu.VMEM((PARTS, ND, CH, KW), f32),
            pltpu.VMEM((PARTS, ND, CH, KW), f32),
            pltpu.VMEM((PARTS, NROW, ND, CH, KW), f32),
            pltpu.VMEM((NX, 2, KW, COLS), f32),
            pltpu.VMEM((ND, KW, COLS), jnp.bfloat16),
            pltpu.VMEM((ND, KW, COLS), jnp.bfloat16),
            pltpu.VMEM((KW, COLS), f32),
            pltpu.VMEM((KW, COLS), f32),
            pltpu.VMEM((KW, COLS), f32),
            dma((PARTS,)),
            dma((PARTS,)),
            dma((PARTS, 2)),
            dma((PARTS, 2)),
            dma((3, 2)),
            dma((NX, 2)),
            dma((3 + PARTS,)),
            dma((PARTS, 4)),
            dma((PARTS, NROW, 2)),
            dma((5,)),
            dma((5,)),
        ],
        compiler_params=pltpu.CompilerParams(
            collective_id=0, has_side_effects=True, vmem_limit_bytes=48 * 1024 * 1024
        ),
    )(*(pltpu.with_memory_space_constraint(a, pltpu.HBM) for a in operands))
    return 2.0 * previous - total


def solution(mesh):
    return jax.shard_map(
        shards,
        mesh=mesh,
        in_specs=(P("row", "col", None), P("col", "row"), P("col", "row"), P(), P("col", None)),
        out_specs=P("col", "row"),
        check_vma=False,
    )
```

```python
import jax
import jax.numpy as jnp
from jax import lax
from jax.experimental import pallas as pl
from jax.experimental.pallas import tpu as pltpu
from jax.sharding import PartitionSpec as P

NY, NZ, NC = 2, 8, 2
NROW = NY * NZ * NC
NH, NX = 2, 4
ND = 6
KW = 512
COLS = 256
PARTS = 2
CH = KW // NROW // PARTS
TURN = (3, 1)
QUAD = NY * NC * CH
SPAN = NZ * QUAD
HALF = ND // 2


def chunk_of(zz, yy, cc):
    return (zz * NY + yy) * NC + cc


def row_of(zz, yy, cc):
    return (yy * NZ + zz) * NC + cc


def kernel(
    offsets_hbm,
    owners_hbm,
    left,
    right,
    out,
    offsets,
    owners,
    spread_first,
    spread_second,
    chosen,
    partner_chosen,
    gathered,
    rights,
    right_hi,
    right_lo,
    own_sum,
    send_par,
    recv_par,
    spread_send,
    spread_recv,
    swap_send,
    swap_recv,
    right_send,
    right_recv,
    local_sem,
    gather_send,
    gather_recv,
    par_send,
    par_recv,
):
    spread = (spread_first, spread_second)
    row = lax.axis_index("row")
    col = lax.axis_index("col")
    y = row // (NZ * NC)
    z = (row // NC) % NZ
    c = row % NC
    h = col // NX
    x = col % NX
    mine = chunk_of(z, y, c)
    east = h * NX + (x + 1) % NX
    west = h * NX + (x + NX - 1) % NX
    partner = (1 - h) * NX + x
    x_west = (x + NX - 1) % NX
    x_east = (x + 1) % NX
    x_far = (x + 2) % NX

    local_right = pltpu.make_async_copy(right, rights.at[x], local_sem.at[0])
    local_right.start()
    tables = []
    for number, (source, target) in enumerate(((offsets_hbm, offsets), (owners_hbm, owners))):
        copy = pltpu.make_async_copy(source, target, local_sem.at[1 + PARTS + number])
        copy.start()
        tables.append(copy)
    local_left = []
    for part in range(PARTS):
        begin = pl.multiple_of(part * SPAN + mine * CH, CH)
        copy = pltpu.make_async_copy(
            left.at[0, pl.ds(begin, CH)], spread[part].at[row], local_sem.at[1 + part]
        )
        copy.start()
        local_left.append(copy)

    barrier = pltpu.get_barrier_semaphore()

    def greet(step, carry):
        pl.semaphore_signal(barrier, inc=1, device_id={"row": (row + step) % NROW})
        return carry

    lax.fori_loop(1, NROW, greet, 0)
    for where in (east, west, partner):
        pl.semaphore_signal(barrier, inc=1, device_id={"col": where})
    pl.semaphore_wait(barrier, NROW - 1 + 3)

    def right_copy(source_ref, owner, slot, way, where):
        return pltpu.make_async_remote_copy(
            src_ref=source_ref,
            dst_ref=rights.at[owner, slot],
            send_sem=right_send.at[way, slot],
            recv_sem=right_recv.at[owner, slot],
            device_id={"col": where},
        )

    def right_wait(owner, slot):
        right_copy(rights.at[owner, slot], owner, slot, 0, east).wait_recv()

    first = []
    for slot_east, slot_west in ((0, 1), (1, 0)):
        for way, slot, where in ((0, slot_east, east), (1, slot_west, west)):
            copy = right_copy(right.at[slot], x, slot, way, where)
            first.append(copy)

    place = y * NZ + z

    def spread_to(part, spot, cc):
        yy = spot // NZ
        zz = spot % NZ
        begin = pl.multiple_of(part * SPAN + chunk_of(zz, yy, cc) * CH, CH)
        pltpu.make_async_remote_copy(
            src_ref=left.at[0, pl.ds(begin, CH)],
            dst_ref=spread[part].at[row],
            send_sem=spread_send.at[part],
            recv_sem=spread_recv.at[part],
            device_id={"row": row_of(zz, yy, cc)},
        ).start()

    def spread_stage(part, cc):
        def spread_start(step, carry):
            spread_to(part, (place + step) % (NY * NZ), cc)
            return carry

        lax.fori_loop(1, NY * NZ, spread_start, 0)

        @pl.when(c != cc)
        def _():
            spread_to(part, place, cc)

    def spread_all(part):
        ref = spread[part].at[pl.ds(0, NROW - 1)]
        return pltpu.make_async_remote_copy(
            src_ref=ref,
            dst_ref=ref,
            send_sem=spread_send.at[part],
            recv_sem=spread_recv.at[part],
            device_id={"col": partner},
        )

    def swap_copy(part, half):
        piece = pl.ds(half * HALF, HALF)
        return pltpu.make_async_remote_copy(
            src_ref=chosen.at[part, piece],
            dst_ref=partner_chosen.at[part, piece],
            send_sem=swap_send.at[part, half],
            recv_sem=swap_recv.at[part, half],
            device_id={"col": partner},
        )

    def crossing(number):
        return ((x + offsets[number] // 2) // NX) % 2

    def choose_stage(part):
        local_left[part].wait()
        spread_all(part).wait_recv()
        for half in (0, 1):
            for number in range(half * HALF, half * HALF + HALF):
                chosen[part, number] = spread[part][owners[0, number]]
            swap_copy(part, half).start()

    beside = {"row": row_of(z, y, 1 - c)}
    across = {"row": row_of(z, 1 - y, c)}
    up = {"row": row_of((z + 1) % NZ, y, c)}
    down = {"row": row_of((z + NZ - 1) % NZ, y, c)}
    BESIDE, ACROSS, UP, DOWN = 0, 1, 2, 3
    targets = {BESIDE: beside, ACROSS: across, UP: up, DOWN: down}
    sent = [{way: 0 for way in targets} for part in range(PARTS)]

    def unit_copy(part, zz, yy, cc, half, way):
        chunk = chunk_of(zz, yy, cc)
        ref = gathered.at[part, chunk, pl.ds(half * HALF, HALF)]
        return pltpu.make_async_remote_copy(
            src_ref=ref,
            dst_ref=ref,
            send_sem=gather_send.at[part, way],
            recv_sem=gather_recv.at[part, chunk, half],
            device_id=targets[way],
        )

    def send(part, zz, yy, cc, half, *ways):
        for way in ways:
            sent[part][way] += 1
            unit_copy(part, zz, yy, cc, half, way).start()

    def receive(part, zz, yy, cc, half):
        unit_copy(part, zz, yy, cc, half, BESIDE).wait_recv()

    def open_units(part):
        def opening(half, *ways):
            def go():
                swap_copy(part, half).wait_recv()
                for number in range(half * HALF, half * HALF + HALF):
                    gathered[part, mine, number] = jnp.where(
                        crossing(number) == 1, partner_chosen[part, number], chosen[part, number]
                    )
                send(part, z, y, c, half, *ways)

            return go

        return [
            opening(0, ACROSS, UP, DOWN, BESIDE),
            opening(1, UP, DOWN, ACROSS, BESIDE),
        ]

    def passing(part, zz, yy, half, *ways):
        def go():
            receive(part, zz, yy, c, half)
            send(part, zz, yy, c, half, *ways)

        return go

    def neighbour_units(part):
        return [passing(part, z, 1 - y, 0, UP, DOWN, BESIDE)]

    def z_units(part, step):
        found = []
        below = (z + NZ - step) % NZ
        above = (z + step) % NZ
        far = step == NZ // 2
        last = step == NZ // 2 - 1
        early = step <= TURN[part]
        units = ((y, 0), (y, 1), (1 - y, 0))
        if not early:
            units += ((1 - y, 1),)
        for yy, half in units:
            extra = (ACROSS, BESIDE) if half == 1 and early else (BESIDE,)
            if not (far and half == 1):
                on = () if far or (last and half == 1) else (UP,)
                found.append(passing(part, below, yy, half, *(on + extra)))
            if not (far and half == 0):
                on = () if far or (last and half == 0) else (DOWN,)
                found.append(passing(part, above, yy, half, *(on + extra)))
        return found

    def places(step):
        if step == 0:
            return (z,)
        if step == NZ // 2:
            return ((z + step) % NZ,)
        return ((z + NZ - step) % NZ, (z + step) % NZ)

    def y_units(part, step):
        found = []
        if step > TURN[part]:
            return found
        for number, zz in enumerate(places(step)):
            on = ()
            if step == TURN[part]:
                if step == 0:
                    on = (UP, DOWN)
                elif number == 1:
                    on = (DOWN,)
                elif step < NZ // 2 - 1:
                    on = (UP,)
            found.append(passing(part, zz, 1 - y, 1, *(on + (BESIDE,))))
        return found

    def prepare_right():
        local_right.wait()
        right_wait(x_west, 1)
        right_wait(x_east, 0)
        right_wait(x_far, 0)
        right_wait(x_far, 1)

        def prepare(number, carry):
            off = offsets[number]
            block = rights[(x + off // 2) % NX, off % 2]
            hi = block.astype(jnp.bfloat16)
            right_hi[number] = hi
            right_lo[number] = (block - hi.astype(jnp.float32)).astype(jnp.bfloat16)
            return carry

        lax.fori_loop(0, ND, prepare, 0)

    def par_copy(index, begin, rows):
        return pltpu.make_async_remote_copy(
            src_ref=send_par.at[pl.ds(begin, rows)],
            dst_ref=recv_par.at[pl.ds(begin, rows)],
            send_sem=par_send.at[index],
            recv_sem=par_recv.at[index],
            device_id={"col": partner},
        )

    def multiply(part, spots, begin, rows, numbers):
        if numbers[0] == 0:
            own_sum[pl.ds(begin, rows)] = jnp.zeros((rows, COLS), jnp.float32)
            send_par[pl.ds(begin, rows)] = jnp.zeros((rows, COLS), jnp.float32)

        def add_term(number, carry):
            pieces = [
                gathered[part, pl.ds(zz * NY * NC, NY * NC), number].reshape(QUAD, KW)
                for zz in spots
            ]
            block = jnp.concatenate(pieces, axis=0)
            hi = block.astype(jnp.bfloat16)
            lo = (block - hi.astype(jnp.float32)).astype(jnp.bfloat16)
            both = jnp.concatenate([hi, lo], axis=0)
            twice = jnp.dot(both, right_hi[number], preferred_element_type=jnp.float32)
            term = jnp.dot(hi, right_lo[number], preferred_element_type=jnp.float32)
            term += twice[:rows] + twice[rows:]
            zero = jnp.zeros_like(term)
            crossed = crossing(number) == 1
            own_sum[pl.ds(begin, rows)] += jnp.where(crossed, zero, term)
            send_par[pl.ds(begin, rows)] += jnp.where(crossed, term, zero)
            return carry

        lax.fori_loop(*numbers, add_term, 0)

    def wait_beside(part, spots):
        for zz in spots:
            for yy in (0, 1):
                for half in (0, 1):
                    receive(part, zz, yy, 1 - c, half)

    def spots_of(*steps):
        return [spot for step in steps for spot in places(step)]

    jobs = []
    for part, steps in ((0, (0, 1, 2)), (0, (3, 4)), (1, (0, 1)), (1, (2, 3)), (1, (4,))):
        begin = jobs[-1][2] + jobs[-1][3] if jobs else 0
        spots = spots_of(*steps)
        jobs.append((part, spots, begin, len(spots) * QUAD))

    def multiply_units(job, slices=1):
        part, spots, begin, rows = jobs[job]
        size = ND // slices

        def piece(index):
            def go():
                if index == 0:
                    wait_beside(part, spots)
                multiply(part, spots, begin, rows, (index * size, index * size + size))
                if index == slices - 1:
                    par_copy(job, begin, rows).start()

            return go

        return [piece(index) for index in range(slices)]

    def by_core(zero, one):
        before = [dict(counts) for counts in sent]

        @pl.when(c == 0)
        def _():
            zero()

        for counts, saved in zip(sent, before):
            counts.update(saved)

        @pl.when(c == 1)
        def _():
            one()

    def run(*lists):
        longest = max(len(units) for units in lists)
        for turn in range(longest):
            for units in lists:
                first_unit = -(-turn * len(units) // longest)
                last_unit = -(-(turn + 1) * len(units) // longest)
                for unit in units[first_unit:last_unit]:
                    unit()

    def finish_stage(job):
        part, spots, begin, rows = jobs[job]
        par_copy(job, begin, rows).wait_recv()
        for number, zz in enumerate(spots):
            piece = pl.ds(begin + number * QUAD, QUAD)
            place = pl.multiple_of(part * SPAN + zz * QUAD, QUAD)
            out[pl.ds(place, QUAD)] = own_sum[piece] + recv_par[piece]

    for copy in first:
        copy.start()
    spread_stage(0, 0)
    spread_stage(0, 1)

    @pl.when(c == 1)
    def _():
        spread_stage(1, 0)

    for copy in tables:
        copy.wait()
    choose_stage(0)

    @pl.when(c == 0)
    def _():
        spread_stage(1, 0)

    spread_stage(1, 1)
    run(open_units(0))
    right_wait(x_west, 0)
    relay_east = right_copy(rights.at[x_west, 0], x_west, 0, 2, east)
    relay_east.start()
    right_wait(x_east, 1)
    relay_west = right_copy(rights.at[x_east, 1], x_east, 1, 2, west)
    relay_west.start()
    run(neighbour_units(0))
    choose_stage(1)

    def zero():
        run(open_units(1))
        run(z_units(0, 1), y_units(0, 0))

    def one():
        run(z_units(0, 1), y_units(0, 0))
        run(open_units(1))

    by_core(zero, one)
    run(z_units(0, 2), y_units(0, 1))
    run(neighbour_units(1))
    run(y_units(0, 2))
    run(z_units(0, 3), z_units(1, 1), y_units(1, 0))
    run(y_units(1, 1), y_units(0, 3))
    prepare_right()
    run(multiply_units(0, 3), z_units(1, 2))
    run(z_units(0, 4), multiply_units(2, 3))
    run(z_units(1, 3), multiply_units(1, 3))
    run(multiply_units(3, 3), z_units(1, 4))
    run(multiply_units(4))
    for job in range(len(jobs)):
        finish_stage(job)

    for copy in first + [relay_east, relay_west]:
        copy.wait_send()
    for part in range(PARTS):
        spread_all(part).wait_send()
        for half in (0, 1):
            swap_copy(part, half).wait_send()
        for way in targets:
            ref = gathered.at[part, pl.ds(0, sent[part][way]), pl.ds(0, HALF)]
            pltpu.make_async_remote_copy(
                src_ref=ref,
                dst_ref=ref,
                send_sem=gather_send.at[part, way],
                recv_sem=gather_recv.at[part, 0, 0],
                device_id=targets[way],
            ).wait_send()
    for index, (part, spots, begin, rows) in enumerate(jobs):
        par_copy(index, begin, rows).wait_send()


def shards(left_slots, right, previous, offsets, owners):
    f32 = jnp.float32
    vmem = pl.BlockSpec(memory_space=pltpu.VMEM)
    hbm = pl.BlockSpec(memory_space=pltpu.HBM)
    dma = pltpu.SemaphoreType.DMA
    operands = (offsets, owners, left_slots, right.reshape(2, KW, COLS))
    total = pl.pallas_call(
        kernel,
        out_shape=jax.ShapeDtypeStruct((KW, COLS), f32),
        in_specs=[hbm] * 4,
        out_specs=vmem,
        scratch_shapes=[
            pltpu.SMEM((ND,), jnp.int32),
            pltpu.SMEM((1, ND), jnp.int32),
            pltpu.VMEM((NROW, CH, KW), f32),
            pltpu.VMEM((NROW, CH, KW), f32),
            pltpu.VMEM((PARTS, ND, CH, KW), f32),
            pltpu.VMEM((PARTS, ND, CH, KW), f32),
            pltpu.VMEM((PARTS, NROW, ND, CH, KW), f32),
            pltpu.VMEM((NX, 2, KW, COLS), f32),
            pltpu.VMEM((ND, KW, COLS), jnp.bfloat16),
            pltpu.VMEM((ND, KW, COLS), jnp.bfloat16),
            pltpu.VMEM((KW, COLS), f32),
            pltpu.VMEM((KW, COLS), f32),
            pltpu.VMEM((KW, COLS), f32),
            dma((PARTS,)),
            dma((PARTS,)),
            dma((PARTS, 2)),
            dma((PARTS, 2)),
            dma((3, 2)),
            dma((NX, 2)),
            dma((3 + PARTS,)),
            dma((PARTS, 4)),
            dma((PARTS, NROW, 2)),
            dma((5,)),
            dma((5,)),
        ],
        compiler_params=pltpu.CompilerParams(
            collective_id=0, has_side_effects=True, vmem_limit_bytes=48 * 1024 * 1024
        ),
    )(*(pltpu.with_memory_space_constraint(a, pltpu.HBM) for a in operands))
    return 2.0 * previous - total


def solution(mesh):
    return jax.shard_map(
        shards,
        mesh=mesh,
        in_specs=(P("row", "col", None), P("col", "row"), P("col", "row"), P(), P("col", None)),
        out_specs=P("col", "row"),
        check_vma=False,
    )
```
